32 devices in a mesh: dp: 8 (over z, x), mix: 4 (over y, core).
Axes of the slice: x: 2, y: 2, z: 4, core: 2. Of those that a mesh axis runs over, the one named last changes fastest.
Arguments:
- inputs: bfloat16 [40, 1280, 768], P('dp', 'mix'), may hold values from -6 to 6
- pass_count: int32 [40], P('dp'), may hold values from 2 to 5
- pass_embed: bfloat16 [5, 768], replicated, may hold values from -3 to 3
- ln1_gain: bfloat16 [768], replicated, may hold values from 0.5 to 1.5
- ln1_bias: bfloat16 [768], replicated, may hold values from -0.59765625 to 0.59765625
- w_qkv: bfloat16 [768, 2304], replicated, may hold values from -0.21875 to 0.21875
- bias_q: bfloat16 [768], replicated, may hold values from -0.59765625 to 0.59765625
- bias_v: bfloat16 [768], replicated, may hold values from -0.29882812 to 0.29882812
- w_out: bfloat16 [768, 768], replicated, may hold values from -3.5 to 3.5
- bias_out: bfloat16 [768], replicated, may hold values from -0.59765625 to 0.59765625
- ln2_gain: bfloat16 [768], replicated, may hold values from 0.5 to 1.5
- ln2_bias: bfloat16 [768], replicated, may hold values from -0.59765625 to 0.59765625
- w_up: bfloat16 [768, 3072], replicated, may hold values from -0.21875 to 0.21875
- bias_up: bfloat16 [3072], replicated, may hold values from -0.59765625 to 0.59765625
- w_down: bfloat16 [3072, 768], replicated, may hold values from -0.21875 to 0.21875
- bias_down: bfloat16 [768], replicated, may hold values from -0.59765625 to 0.59765625
- cotangent: bfloat16 [40, 1280, 768], P('dp', 'mix'), may hold values from -6 to 6
Outputs:
- out: float32 [40, 1280, 768], P('dp', 'mix')
- grad_x: float32 [40, 1280, 768], P('dp', 'mix')
- grad_pass_embed: float32 [5, 768], replicated
- grad_ln1_gain: float32 [768], replicated
- grad_ln1_bias: float32 [768], replicated
- grad_w_qkv: float32 [768, 2304], P('dp', 'mix')
- grad_bias_q: float32 [768], replicated
- grad_bias_v: float32 [768], replicated
- grad_w_out: float32 [768, 768], P('dp', 'mix')
- grad_bias_out: float32 [768], replicated
- grad_ln2_gain: float32 [768], replicated
- grad_ln2_bias: float32 [768], replicated
- grad_w_up: float32 [768, 3072], P('dp', 'mix')
- grad_bias_up: float32 [3072], replicated
- grad_w_down: float32 [3072, 768], P('dp', 'mix')
- grad_bias_down: float32 [768], replicated
The draws below stay inside these ranges and needn't reach their ends.
Inputs may be any that keep to these rules, and one draw needn't show every extreme that they name: Item i uses passes 0 to pass_count[i] - 1 of each token; the other slots are masked.
All inputs are finite; a program needn't handle non-finite values.
Results may differ from the reference program's by a relative error of at most 0.0095.
Values may be sent and summed in bfloat16 or wider, within the bound.
No kernel may reach another device: no remote copies, remote signals or barrier semaphores. Data moves between devices by JAX's collectives and lax.ppermute only.
A program may use at most 256 MiB of HBM per device.

```python
import math
import jax
import jax.numpy as jnp
from jax import lax

D = 768
HEADS = 12
HEAD = 64
FF = 3072
PASSES = 5
ITEMS = 40
SLOTS = 1280


def touch_ends(values, rng, smallest, largest):
    longest = values.shape.index(max(values.shape))
    spots = []
    for shift in (0, 1):
        where = [jax.random.randint(jax.random.fold_in(rng, axis), (), 0, length) for axis, length in enumerate(values.shape)]
        where[longest] = (where[longest] + shift) % values.shape[longest]
        spots.append(tuple(where))
    return values.at[spots[0]].set(smallest).at[spots[1]].set(largest)


def with_spikes(entries, key, source, target, parts, factor):
    def block_of(dim):
        return (jnp.arange(entries.shape[dim]) // (entries.shape[dim] // parts)).reshape((-1,) + (1,) * (entries.ndim - 1 - dim))

    one_side = jax.random.permutation(key, parts)[block_of(target)]
    far = (block_of(target) + parts // 2) % parts
    return jnp.where((block_of(source) == one_side) | (block_of(source) == far), factor * entries, entries)


def shard_levels(rng, extent, split, low, largest):
    level = 1.0
    for position, parts in split:
        steps = jax.random.uniform(jax.random.fold_in(jax.random.fold_in(rng, 6), position), (parts,), jnp.float32, low / len(split), largest / len(split))
        level = level * jnp.repeat(jnp.exp(steps), extent[position] // parts).reshape((-1,) + (1,) * (len(extent) - 1 - position))
    return level


def gaussian(stream_key, extent, scale, bound, pieces=(), held_as=jnp.bfloat16):
    factor_of = shard_levels(stream_key, extent, pieces, -0.22, 0.18) if pieces else 1.0
    drawn = jax.random.normal(stream_key, extent, jnp.float32) * scale * factor_of
    return jnp.minimum(jnp.maximum(drawn, -bound), bound).astype(held_as)


def heavy_noise(rng, shape, width, bound, shards, heavy, kind=jnp.bfloat16):
    array = width * jax.random.normal(rng, shape, jnp.float32)
    if shards:
        array = array * shard_levels(rng, shape, shards, -0.22, 0.18)
    return jnp.clip(with_spikes(array, jax.random.fold_in(rng, 3), *heavy), -bound, bound).astype(kind)


def setup_inputs(seed: int = 0) -> dict:
    streams_of = jax.random.split(jax.random.key(seed), 18)
    inputs = gaussian(streams_of[0], (ITEMS, SLOTS, D), 1.0, 6.0, ((0, 8), (1, 4)))
    pass_count = touch_ends(jax.random.randint(streams_of[1], (ITEMS,), 2, PASSES + 1), jax.random.fold_in(streams_of[1], 1), 2, PASSES).astype(jnp.int32)
    pass_embed = gaussian(streams_of[2], (PASSES, D), 0.5, 3.0)
    ln1_gain = jnp.clip(1.0 + 0.1 * jax.random.normal(streams_of[3], (D,), jnp.float32), 0.5, 1.5).astype(jnp.bfloat16)
    ln1_bias = gaussian(streams_of[4], (D,), 0.1, 0.59765625)
    w_qkv = gaussian(streams_of[5], (D, 3 * D), D ** -0.5, 0.21875)
    bias_q = gaussian(streams_of[6], (D,), 0.1, 0.59765625)
    bias_v = gaussian(streams_of[7], (D,), 0.05, 0.29882812)
    w_out = gaussian(streams_of[8], (D, D), (max(1, D // 256)) ** -0.5, 3.5)
    bias_out = gaussian(streams_of[9], (D,), 0.1, 0.59765625)
    ln2_gain = jnp.clip(1.0 + 0.1 * jax.random.normal(streams_of[10], (D,), jnp.float32), 0.5, 1.5).astype(jnp.bfloat16)
    ln2_bias = gaussian(streams_of[11], (D,), 0.1, 0.59765625)
    w_up = gaussian(streams_of[12], (D, FF), D ** -0.5, 0.21875)
    bias_up = gaussian(streams_of[13], (FF,), 0.1, 0.59765625)
    w_down = gaussian(streams_of[14], (FF, D), (FF // 4) ** -0.5, 0.21875)
    bias_down = gaussian(streams_of[15], (D,), 0.1, 0.59765625)
    cotangent = heavy_noise(streams_of[16], (ITEMS, SLOTS, D), 1.0, 6.0, ((0, 8), (1, 4)), (0, 2, 8, 2.0))
    return dict(inputs=inputs, pass_count=pass_count, pass_embed=pass_embed, ln1_gain=ln1_gain, ln1_bias=ln1_bias, w_qkv=w_qkv, bias_q=bias_q, bias_v=bias_v, w_out=w_out, bias_out=bias_out, ln2_gain=ln2_gain, ln2_bias=ln2_bias, w_up=w_up, bias_up=bias_up, w_down=w_down, bias_down=bias_down, cotangent=cotangent)


@jax.custom_vjp
def low(v):
    return lax.optimization_barrier(v.astype(jnp.bfloat16)).astype(jnp.float32)

@jax.custom_vjp
def low_back(v):
    return v

def low_keep(v):
    return (low(v), None)

def low_pass(kept, grad):
    return (grad,)

def back_keep(v):
    return (v, None)

def back_low(kept, grad):
    return (low(grad),)
low.defvjp(low_keep, low_pass)
low_back.defvjp(back_keep, back_low)
epsilon = 1e-05
highest = lax.Precision.HIGHEST

def layer_norm(values, gain_vec, shift_vec):
    center = values - lax.optimization_barrier(jnp.mean(values, axis=-1, keepdims=True))
    inverse = lax.rsqrt(lax.optimization_barrier(jnp.mean(center * center, axis=-1, keepdims=True)) + epsilon)
    return center * inverse * gain_vec + shift_vec

def forward_item(inputs_item, passes_item, params):
    pass_embed, ln1_gain, ln1_bias, w_qkv, bias_q, bias_v, w_out, bias_out, ln2_gain, ln2_bias, w_up, bias_up, w_down, bias_down = params
    slot_ids = jnp.arange(SLOTS, dtype=jnp.int32)
    pass_ids = slot_ids % PASSES
    onehot = (pass_ids[:, None] == jnp.arange(PASSES, dtype=jnp.int32)[None, :]).astype(jnp.float32)
    keep_mask = (pass_ids < passes_item).astype(jnp.float32)[:, None]
    hidden = inputs_item + jnp.dot(onehot, pass_embed, precision=highest)
    first_low = low(layer_norm(hidden, ln1_gain, ln1_bias))
    joined = jnp.dot(first_low, w_qkv, precision=highest)
    queries = low_back(low(joined[:, :D] + bias_q)).reshape(SLOTS, HEADS, HEAD)
    key_rows = low_back(low(joined[:, D:2 * D])).reshape(SLOTS, HEADS, HEAD)
    value_rows = low_back(low(joined[:, 2 * D:] + bias_v)).reshape(SLOTS, HEADS, HEAD)
    raw_scores = jnp.einsum('qhd,khd->hqk', queries, key_rows, precision=highest)
    scores = low_back(raw_scores * (1.0 / math.sqrt(HEAD)))
    allowed = (slot_ids[None, :] <= slot_ids[:, None]) & (pass_ids[None, :] < passes_item)
    scores = jnp.where(allowed[None], scores, -1e+30)
    probs = jax.nn.softmax(scores, axis=-1)
    attended = jnp.einsum('hqk,khd->qhd', low(probs), value_rows, precision=highest).reshape(SLOTS, D)
    attended = low_back(low(attended))
    attn_out = low_back(jnp.dot(attended, w_out, precision=highest) + bias_out)
    mixed_rows = hidden + keep_mask * attn_out
    second_low = low(layer_norm(mixed_rows, ln2_gain, ln2_bias))
    pre_act = low_back(jnp.dot(second_low, w_up, precision=highest) + bias_up)
    act_low = low(jax.nn.gelu(pre_act, approximate=True))
    branch = low_back(jnp.dot(act_low, w_down, precision=highest) + bias_down)
    return mixed_rows + keep_mask * branch

def reference(inputs, pass_count, pass_embed, ln1_gain, ln1_bias, w_qkv, bias_q, bias_v, w_out, bias_out, ln2_gain, ln2_bias, w_up, bias_up, w_down, bias_down, cotangent):
    params = tuple((weight.astype(jnp.float32) for weight in (pass_embed, ln1_gain, ln1_bias, w_qkv, bias_q, bias_v, w_out, bias_out, ln2_gain, ln2_bias, w_up, bias_up, w_down, bias_down)))

    def one_sample(totals, sample):
        inputs_item, passes_item, grad_item = sample
        result, pullback = jax.vjp(lambda values, weights: forward_item(values, passes_item, weights), inputs_item.astype(jnp.float32), params)
        grad_values, grad_weights = pullback(grad_item.astype(jnp.float32))
        return (jax.tree.map(jnp.add, totals, grad_weights), (result, grad_values))
    starts = jax.tree.map(jnp.zeros_like, params)
    totals, (result, grad_x) = lax.scan(one_sample, starts, (inputs, pass_count, cotangent))
    return (result, grad_x, totals[0], totals[1], totals[2], totals[3], totals[4], totals[5], totals[6], totals[7], totals[8], totals[9], totals[10], totals[11], totals[12], totals[13])
```

```python
import functools
import math

import jax
import jax.numpy as jnp
from jax import lax
from jax.experimental import pallas as pl
from jax.experimental.pallas import tpu as pltpu
from jax.sharding import PartitionSpec as P

HEAD = 64
PASSES = 5
EPS = 1e-05
NEG = -1e30
BF = jnp.bfloat16
F32 = jnp.float32
VMEM_LIMIT = 62 * 1024 * 1024
TILE = 256


def dg(a, b, ca, cb):
    return lax.dot_general(a, b, (((ca,), (cb,)), ((), ())), preferred_element_type=F32)


def params(n=1, limit=VMEM_LIMIT):
    return pltpu.CompilerParams(
        dimension_semantics=("arbitrary",) * n, vmem_limit_bytes=limit
    )


def const_spec(shape):
    zeros = (0,) * len(shape)
    return pl.BlockSpec(shape, lambda *_: zeros, pipeline_mode=pl.Buffered(1))


def cost(flops, nbytes, trans=0):
    return pl.CostEstimate(flops=int(flops), bytes_accessed=int(nbytes), transcendentals=int(trans))


def ln_stats(values):
    center = values - jnp.mean(values, axis=-1, keepdims=True)
    inverse = lax.rsqrt(jnp.mean(center * center, axis=-1, keepdims=True) + EPS)
    return center * inverse, inverse


def ln_back(upstream, normed, inverse, gain):
    scaled = upstream * gain
    inner = scaled - jnp.mean(scaled, axis=-1, keepdims=True)
    inner = inner - normed * jnp.mean(scaled * normed, axis=-1, keepdims=True)
    return inverse * inner


def qkv_body(x_ref, pe_ref, g_ref, b_ref, w_ref, bias_ref, scale_ref, o_ref):
    hidden = x_ref[...].astype(F32) + pe_ref[...].astype(F32)
    normed, _ = ln_stats(hidden)
    low = (normed * g_ref[...] + b_ref[...]).astype(BF)
    out = dg(low, w_ref[...], 1, 0) + bias_ref[...]
    o_ref[...] = (out * scale_ref[...]).astype(BF)


def qkv_whole(x, pe, gain, bias, w, wb, ws):
    rows, width = x.shape
    tile = pe.shape[0]
    cols = w.shape[1]
    return pl.pallas_call(
        qkv_body,
        grid=(rows // tile,),
        in_specs=[
            pl.BlockSpec((tile, width), lambda i: (i, 0)),
            const_spec((tile, width)),
            const_spec((1, width)),
            const_spec((1, width)),
            const_spec((width, cols)),
            const_spec((1, cols)),
            const_spec((1, cols)),
        ],
        out_specs=pl.BlockSpec((tile, cols), lambda i: (i, 0)),
        out_shape=jax.ShapeDtypeStruct((rows, cols), BF),
        compiler_params=params(),
        cost_estimate=cost(2 * rows * width * cols, 2 * (rows * (width + cols) + width * cols)),
        name="qkv_whole",
    )(x, pe, gain, bias, w, wb, ws)


def qkv_split_body(x_ref, pe_ref, g_ref, b_ref, w_ref, bias_ref, scale_ref, o_ref):
    hidden = x_ref[...].astype(F32) + pe_ref[...].astype(F32)
    normed, _ = ln_stats(hidden)
    low = (normed * g_ref[...] + b_ref[...]).astype(BF)
    for part in range(w_ref.shape[0]):
        out = dg(low, w_ref[part], 1, 0) + bias_ref[part]
        o_ref[part] = (out * scale_ref[...]).astype(BF)


def qkv_split(x, pe, gain, bias, w, wb, ws):
    rows, width = x.shape
    parts, _, cols = w.shape
    return pl.pallas_call(
        qkv_split_body,
        out_shape=jax.ShapeDtypeStruct((parts, rows, cols), BF),
        compiler_params=pltpu.CompilerParams(vmem_limit_bytes=VMEM_LIMIT),
        cost_estimate=cost(2 * rows * width * cols * parts, 2 * parts * cols * (rows + width)),
        name="qkv_split",
    )(x, pe, gain, bias, w, wb, ws)


def head_mask(block, half):
    lane = lax.broadcasted_iota(jnp.int32, block.shape, 1)
    return jnp.where((lane // HEAD) == half, block, jnp.zeros_like(block))


def causal(scores):
    row = lax.broadcasted_iota(jnp.int32, scores.shape, 0)
    col = lax.broadcasted_iota(jnp.int32, scores.shape, 1)
    return jnp.where(row <= col, scores, NEG)


def score_tile(k, q_tile, kb, lo, hi):
    s = dg(k[:hi], q_tile, 1, 1)
    s = s + kb[:hi]
    if lo:
        return jnp.concatenate([s[:lo], causal(s[lo:])], axis=0)
    return causal(s)


def forward_heads(keys, queries, vt_ref, kb_ref, lse_ref, store):
    slots = keys[0].shape[0]
    count = len(queries)
    for lo in range(0, slots, TILE):
        hi = lo + TILE
        outs = []
        for h in range(count):
            s = score_tile(keys[h], queries[h][lo:hi], kb_ref, lo, hi)
            top = jnp.max(s, axis=0, keepdims=True)
            p = jnp.exp(s - top).astype(BF)
            o = dg(vt_ref[h, :, :hi], p, 1, 0)
            total = o[HEAD : HEAD + 1]
            outs.append(o[:HEAD] * (1.0 / total))
            lse_ref[h : h + 1, lo:hi] = top + jnp.log(total)
        store(lo, hi, jnp.concatenate(outs, axis=0).T.astype(BF))


def fill_vt(vt_ref, value_block, count):
    vt = value_block.T
    for h in range(count):
        vt_ref[h, :HEAD, :] = vt[h * HEAD : (h + 1) * HEAD]
        vt_ref[h, HEAD:, :] = jnp.ones((16, vt.shape[1]), BF)


def attend_whole_body(q_ref, k_ref, v_ref, kb_ref, o_ref, lse_ref, vt_ref):
    q = q_ref[...]
    k = k_ref[...]
    fill_vt(vt_ref, v_ref[...], 2)

    def store(lo, hi, value):
        o_ref[lo:hi, :] = value

    forward_heads([k, k], [head_mask(q, 0), head_mask(q, 1)], vt_ref, kb_ref, lse_ref.at[0], store)


def attend_whole(qkv, kb):
    slots, cols = qkv.shape
    width = cols // 3
    pairs = width // (2 * HEAD)
    block = lambda off: pl.BlockSpec((slots, 2 * HEAD), lambda j: (0, off * pairs + j))
    area = slots * slots * 0.6
    return pl.pallas_call(
        attend_whole_body,
        grid=(pairs,),
        in_specs=[block(0), block(1), block(2), const_spec(kb.shape)],
        out_specs=[block(0), pl.BlockSpec((1, 8, slots), lambda j: (j, 0, 0))],
        out_shape=[
            jax.ShapeDtypeStruct((slots, width), BF),
            jax.ShapeDtypeStruct((pairs, 8, slots), F32),
        ],
        scratch_shapes=[pltpu.VMEM((2, HEAD + 16, slots), BF)],
        compiler_params=params(),
        cost_estimate=cost(8 * area * width * 4, 8 * slots * width, area * pairs * 2),
        name="attend_whole",
    )(qkv, qkv, qkv, kb)


def cut(block, part, h, count):
    base = (part * count + h) * HEAD
    return block[:, base : base + HEAD]


def attend_split_body(qkv_ref, kb_ref, o_ref, lse_ref, vt_ref):
    block = qkv_ref[...]
    count = block.shape[1] // (3 * HEAD)
    fill_vt(vt_ref, block[:, 2 * count * HEAD :], count)

    def store(lo, hi, value):
        o_ref[lo:hi, :] = value

    keys = [cut(block, 1, h, count) for h in range(count)]
    queries = [cut(block, 0, h, count) for h in range(count)]
    forward_heads(keys, queries, vt_ref, kb_ref, lse_ref, store)


def attend_split(qkv, kb):
    slots, cols = qkv.shape
    count = cols // (3 * HEAD)
    area = slots * slots * 0.6
    return pl.pallas_call(
        attend_split_body,
        out_shape=[
            jax.ShapeDtypeStruct((slots, count * HEAD), BF),
            jax.ShapeDtypeStruct((8, slots), F32),
        ],
        scratch_shapes=[pltpu.VMEM((count, HEAD + 16, slots), BF)],
        compiler_params=pltpu.CompilerParams(vmem_limit_bytes=VMEM_LIMIT),
        cost_estimate=cost(8 * area * count * HEAD * 4, 8 * slots * cols, area * count),
        name="attend_split",
    )(qkv, kb)


def inner_rows(d_ref, do, o, count):
    prod = (do.astype(F32) * o.astype(F32)).T
    for h in range(count):
        d_ref[h : h + 1, :] = jnp.sum(prod[h * HEAD : (h + 1) * HEAD], axis=0, keepdims=True)


def backward_tile(k, v, kt, q_tile, do_tile, kb_ref, lse_row, d_row, lo, hi):
    s = score_tile(k, q_tile, kb_ref, lo, hi)
    p = jnp.exp(s - lse_row)
    dp = dg(v[:hi], do_tile, 1, 1)
    ds = (p * (dp - d_row)).astype(BF)
    dqt = dg(kt[:, :hi], ds, 1, 0)
    return p.astype(BF), ds, dqt


def back_whole_body(q_ref, k_ref, v_ref, do_ref, o_ref, lse_ref, kb_ref, out_ref, d_ref, kt_ref, dk_ref, dv_ref):
    q, k, v, do = q_ref[...], k_ref[...], v_ref[...], do_ref[...]
    slots = q.shape[0]
    inner_rows(d_ref, do, o_ref[...], 2)
    kt_ref[...] = k.T
    queries = [head_mask(q, h) for h in range(2)]
    grads = [head_mask(do, h) for h in range(2)]
    for lo in reversed(range(0, slots, TILE)):
        hi = lo + TILE
        got = [
            backward_tile(
                k,
                v,
                kt_ref[h * HEAD : (h + 1) * HEAD, :],
                queries[h][lo:hi],
                grads[h][lo:hi],
                kb_ref,
                lse_ref[0, h : h + 1, lo:hi],
                d_ref[h : h + 1, lo:hi],
                lo,
                hi,
            )
            for h in range(2)
        ]
        dv = dg(
            jnp.concatenate([got[0][0], got[1][0]], axis=1),
            jnp.concatenate([grads[0][lo:hi], grads[1][lo:hi]], axis=0),
            1,
            0,
        )
        dk = dg(
            jnp.concatenate([got[0][1], got[1][1]], axis=1),
            jnp.concatenate([queries[0][lo:hi], queries[1][lo:hi]], axis=0),
            1,
            0,
        )
        if hi == slots:
            dv_ref[...] = dv
            dk_ref[...] = dk
        else:
            dv_ref[:hi, :] += dv
            dk_ref[:hi, :] += dk
        dqt = jnp.concatenate([got[0][2], got[1][2]], axis=0)
        out_ref[0, lo:hi, :] = (dqt.T * (1.0 / math.sqrt(HEAD))).astype(BF)
    out_ref[1] = dk_ref[...].astype(BF)
    out_ref[2] = dv_ref[...].astype(BF)


def back_whole(qkv, do, att, lse, kb):
    slots, cols = qkv.shape
    width = cols // 3
    pairs = width // (2 * HEAD)
    block = lambda off: pl.BlockSpec((slots, 2 * HEAD), lambda j: (0, off * pairs + j))
    area = slots * slots * 0.6
    return pl.pallas_call(
        back_whole_body,
        grid=(pairs,),
        in_specs=[
            block(0),
            block(1),
            block(2),
            block(0),
            block(0),
            pl.BlockSpec((1, 8, slots), lambda j: (j, 0, 0)),
            const_spec(kb.shape),
        ],
        out_specs=pl.BlockSpec((3, slots, 2 * HEAD), lambda j: (0, 0, j)),
        out_shape=jax.ShapeDtypeStruct((3, slots, width), BF),
        scratch_shapes=[
            pltpu.VMEM((8, slots), F32),
            pltpu.VMEM((2 * HEAD, slots), BF),
            pltpu.VMEM((slots, 2 * HEAD), F32),
            pltpu.VMEM((slots, 2 * HEAD), F32),
        ],
        compiler_params=params(),
        cost_estimate=cost(20 * area * width * 4, 16 * slots * width, area * pairs * 2),
        name="back_whole",
    )(qkv, qkv, qkv, do, att, lse, kb)


def back_split_body(qkv_ref, do_ref, o_ref, lse_ref, kb_ref, out_ref, d_ref, kt_ref, dk_ref, dv_ref):
    block, do = qkv_ref[...], do_ref[...]
    slots = block.shape[0]
    count = block.shape[1] // (3 * HEAD)
    wide = count * HEAD
    inner_rows(d_ref, do, o_ref[...], count)
    kt_ref[...] = block[:, wide : 2 * wide].T
    queries = [cut(block, 0, h, count) for h in range(count)]
    keys = [cut(block, 1, h, count) for h in range(count)]
    values = [cut(block, 2, h, count) for h in range(count)]
    grads = [do[:, h * HEAD : (h + 1) * HEAD] for h in range(count)]
    for lo in reversed(range(0, slots, TILE)):
        hi = lo + TILE
        dqts = []
        for h in range(count):
            p, ds, dqt = backward_tile(
                keys[h],
                values[h],
                kt_ref[h * HEAD : (h + 1) * HEAD, :],
                queries[h][lo:hi],
                grads[h][lo:hi],
                kb_ref,
                lse_ref[h : h + 1, lo:hi],
                d_ref[h : h + 1, lo:hi],
                lo,
                hi,
            )
            dqts.append(dqt)
            dv = dg(p, grads[h][lo:hi], 1, 0)
            dk = dg(ds, queries[h][lo:hi], 1, 0)
            if hi == slots:
                dv_ref[h] = dv
                dk_ref[h] = dk
            else:
                dv_ref[h, :hi, :] += dv
                dk_ref[h, :hi, :] += dk
        dqt = jnp.concatenate(dqts, axis=0)
        out_ref[lo:hi, :wide] = (dqt.T * (1.0 / math.sqrt(HEAD))).astype(BF)
    for h in range(count):
        out_ref[:, wide + h * HEAD : wide + (h + 1) * HEAD] = dk_ref[h].astype(BF)
        out_ref[:, 2 * wide + h * HEAD : 2 * wide + (h + 1) * HEAD] = dv_ref[h].astype(BF)


def back_split(qkv, do, att, lse, kb):
    slots, cols = qkv.shape
    count = cols // (3 * HEAD)
    area = slots * slots * 0.6
    return pl.pallas_call(
        back_split_body,
        out_shape=jax.ShapeDtypeStruct((slots, cols), BF),
        scratch_shapes=[
            pltpu.VMEM((8, slots), F32),
            pltpu.VMEM((count * HEAD, slots), BF),
            pltpu.VMEM((count, slots, HEAD), F32),
            pltpu.VMEM((count, slots, HEAD), F32),
        ],
        compiler_params=pltpu.CompilerParams(vmem_limit_bytes=VMEM_LIMIT),
        cost_estimate=cost(20 * area * count * HEAD * 4, 8 * slots * cols, area * count),
        name="back_split",
    )(qkv, do, att, lse, kb)


def mlp_body(
    xm_ref,
    x4_ref,
    cm_ref,
    c4_ref,
    am_ref,
    a4_ref,
    pe_ref,
    keep_ref,
    wo_ref,
    bo_ref,
    g2_ref,
    b2_ref,
    bd_ref,
    wu_ref,
    bu_ref,
    wd_ref,
    outm_ref,
    out4_ref,
    gmm_ref,
    gm4_ref,
    dam_ref,
    da4_ref,
    gwu_ref,
    gwd_ref,
    gwo_ref,
    gbu_ref,
    small_ref,
    mixed_ref,
    acc_ref,
    gsl_ref,
    sl_ref,
    gm_ref,
    slt_ref,
    gmt_ref,
    att_ref,
    gbd_ref,
    act_ref,
    gp_ref,
):
    step = pl.program_id(0)
    last = pl.num_programs(0) - 1
    tile = pe_ref.shape[0]
    rows = mixed_ref.shape[0]
    whole_tiles = xm_ref.shape[0] // tile
    parts = a4_ref.shape[0]
    piece = a4_ref.shape[2]

    def prologue(row, x, cot, keep, att):
        hidden = x.astype(F32) + pe_ref[...].astype(F32)
        mixed = hidden + keep * (dg(att, wo_ref[...], 1, 0) + bo_ref[...])
        mixed_ref[pl.ds(row, tile), :] = mixed
        normed, _ = ln_stats(mixed)
        sl_ref[pl.ds(row, tile), :] = (normed * g2_ref[...] + b2_ref[...]).astype(BF)
        gm = keep * cot.astype(F32)
        gm_ref[pl.ds(row, tile), :] = gm.astype(BF)
        gbd_ref[...] += jnp.sum(gm, axis=0, keepdims=True)

    @pl.when(step == 0)
    def _():
        gbd_ref[...] = jnp.zeros_like(gbd_ref)
        for part in range(parts):
            att_ref[:, part * piece : (part + 1) * piece] = a4_ref[part]

        def loop(i, carry):
            row = pl.multiple_of(i * tile, tile)
            prologue(
                row,
                xm_ref[pl.ds(row, tile), :],
                cm_ref[pl.ds(row, tile), :],
                keep_ref[:, 0:1],
                am_ref[pl.ds(row, tile), :],
            )
            return carry

        lax.fori_loop(0, whole_tiles, loop, 0)
        prologue(whole_tiles * tile, x4_ref[...], c4_ref[...], keep_ref[:, 1:2], att_ref[...])
        slt_ref[...] = sl_ref[...].T
        gmt_ref[...] = gm_ref[...].T

    @pl.when(step == 0)
    def _():
        acc_ref[...] = jnp.zeros_like(acc_ref)
        gsl_ref[...] = jnp.zeros_like(gsl_ref)

    root = math.sqrt(2.0 / math.pi)
    bias_sum = jnp.zeros(bu_ref.shape, F32)
    half_rows = rows // 2
    for part in range(2):
        span = pl.ds(part * half_rows, half_rows)
        pre = dg(sl_ref[span, :], wu_ref[...], 1, 0) + bu_ref[...]
        square = pre * pre
        tanh = jnp.tanh(root * pre * (1.0 + 0.044715 * square))
        half = 0.5 * (1.0 + tanh)
        act = (pre * half).astype(BF)
        act_ref[span, :] = act
        slope = half + 0.5 * pre * (1.0 - tanh * tanh) * (
            root * (1.0 + (3.0 * 0.044715) * square)
        )
        grad_pre = (dg(gm_ref[span, :], wd_ref[...], 1, 1) * slope).astype(BF)
        gp_ref[span, :] = grad_pre
        bias_sum += jnp.sum(grad_pre.astype(F32), axis=0, keepdims=True)
        acc_ref[span, :] += dg(act, wd_ref[...], 1, 0)
        gsl_ref[span, :] += dg(grad_pre, wu_ref[...], 1, 1)
    gbu_ref[0] = bias_sum

    gwd = dg(gmt_ref[...], act_ref[...], 1, 0).astype(BF)
    shard = gwd_ref.shape[2]
    for part in range(gwd_ref.shape[0]):
        gwd_ref[part, 0] = gwd[part * shard : (part + 1) * shard]
    gwu_ref[0] = dg(slt_ref[...], gp_ref[...], 1, 0).astype(BF)

    def epilogue(row, cot, keep):
        mixed = mixed_ref[pl.ds(row, tile), :]
        out = mixed + keep * (acc_ref[pl.ds(row, tile), :] + bd_ref[...])
        normed, inverse = ln_stats(mixed)
        up = gsl_ref[pl.ds(row, tile), :]
        small_ref[1:2, :] += jnp.sum(up * normed, axis=0, keepdims=True)
        small_ref[2:3, :] += jnp.sum(up, axis=0, keepdims=True)
        grad_mixed = cot.astype(F32) + ln_back(up, normed, inverse, g2_ref[...])
        grad_attn = (keep * grad_mixed).astype(BF)
        gm_ref[pl.ds(row, tile), :] = grad_attn
        small_ref[3:4, :] += jnp.sum(grad_attn.astype(F32), axis=0, keepdims=True)
        return out, grad_mixed.astype(BF), dg(grad_attn, wo_ref[...], 1, 1).astype(BF)

    @pl.when(step == last)
    def _():
        small_ref[...] = jnp.zeros_like(small_ref)
        small_ref[0:1, :] = gbd_ref[...]

        def loop(i, carry):
            row = pl.multiple_of(i * tile, tile)
            out, grad_mixed, grad_att = epilogue(row, cm_ref[pl.ds(row, tile), :], keep_ref[:, 0:1])
            outm_ref[pl.ds(row, tile), :] = out.astype(BF)
            gmm_ref[pl.ds(row, tile), :] = grad_mixed
            dam_ref[pl.ds(row, tile), :] = grad_att
            return carry

        lax.fori_loop(0, whole_tiles, loop, 0)
        base = whole_tiles * tile
        out, grad_mixed, grad_att = epilogue(base, c4_ref[...], keep_ref[:, 1:2])
        out4_ref[...] = out
        gm4_ref[...] = grad_mixed
        for part in range(parts):
            da4_ref[part] = grad_att[:, part * piece : (part + 1) * piece]
        slt_ref[:, :base] = am_ref[...].T
        slt_ref[:, base:] = att_ref[...].T
        gwo = dg(slt_ref[...], gm_ref[...], 1, 0).astype(BF)
        for part in range(parts):
            gwo_ref[part] = gwo[:, part * piece : (part + 1) * piece]


def mlp(xm, x4, cm, c4, am, a4, pe, keep, wo, bo, g2, b2, bd, wu, bu, wd, dp):
    rows_m, width = xm.shape
    rows_4 = x4.shape[0]
    rows = rows_m + rows_4
    wide = wu.shape[1]
    parts = a4.shape[0]
    piece = a4.shape[2]
    chunk = 384
    steps = wide // chunk
    block_cols = wide // parts
    per = block_cols // chunk
    out_shape = [
        jax.ShapeDtypeStruct((rows_m, width), BF),
        jax.ShapeDtypeStruct((rows_4, width), F32),
        jax.ShapeDtypeStruct((rows_m, width), BF),
        jax.ShapeDtypeStruct((rows_4, width), BF),
        jax.ShapeDtypeStruct((rows_m, width), BF),
        jax.ShapeDtypeStruct((parts, rows_4, piece), BF),
        jax.ShapeDtypeStruct((parts, width, block_cols), BF),
        jax.ShapeDtypeStruct((parts, steps, width // parts, chunk), BF),
        jax.ShapeDtypeStruct((parts, width, piece), BF),
        jax.ShapeDtypeStruct((steps, 1, chunk), F32),
        jax.ShapeDtypeStruct((8, width), F32),
    ]
    ins = [xm, x4, cm, c4, am, a4, pe, keep, wo, bo, g2, b2, bd]
    in_specs = [const_spec(a.shape) for a in ins] + [
        pl.BlockSpec((width, chunk), lambda c: (0, c)),
        pl.BlockSpec((1, chunk), lambda c: (0, c)),
        pl.BlockSpec((chunk, width), lambda c: (c, 0)),
    ]
    out_specs = [const_spec(s.shape) for s in out_shape[:6]] + [
        pl.BlockSpec((1, width, chunk), lambda c: (c // per, 0, c % per)),
        pl.BlockSpec((parts, 1, width // parts, chunk), lambda c: (0, c, 0, 0)),
        const_spec(out_shape[8].shape),
        pl.BlockSpec((1, 1, chunk), lambda c: (c, 0, 0)),
        const_spec(out_shape[10].shape),
    ]
    return pl.pallas_call(
        mlp_body,
        grid=(steps,),
        in_specs=in_specs,
        out_specs=out_specs,
        out_shape=out_shape,
        scratch_shapes=[
            pltpu.VMEM((rows, width), F32),
            pltpu.VMEM((rows, width), F32),
            pltpu.VMEM((rows, width), F32),
            pltpu.VMEM((rows, width), BF),
            pltpu.VMEM((rows, width), BF),
            pltpu.VMEM((width, rows), BF),
            pltpu.VMEM((width, rows), BF),
            pltpu.VMEM((rows_4, width), BF),
            pltpu.VMEM((1, width), F32),
            pltpu.VMEM((rows, chunk), BF),
            pltpu.VMEM((rows, chunk), BF),
        ],
        compiler_params=params(),
        cost_estimate=cost(
            12 * rows * width * wide + 6 * rows * width * width, 16 * rows * width, rows * wide
        ),
        name="mlp",
    )(*ins, wu, bu, wd)


def assemble(d4_ref, src_ref):
    parts, _, cols = src_ref.shape
    piece = cols // 3
    width = parts * piece
    for kind in range(3):
        for part in range(parts):
            d4_ref[:, kind * width + part * piece : kind * width + (part + 1) * piece] = src_ref[
                part, :, kind * piece : (kind + 1) * piece
            ]


def wqkv_body(xm_ref, x4_ref, pe_ref, g_ref, b_ref, dm_ref, d4_ref, gw_ref, sums_ref, low_ref, flat_ref, cur_ref):
    tile = pe_ref.shape[0]
    whole_tiles = xm_ref.shape[0] // tile
    base = whole_tiles * tile
    width = xm_ref.shape[1]
    parts = gw_ref.shape[0]
    cols = gw_ref.shape[2]
    rows4, wide = flat_ref.shape

    def first(row, x):
        normed, _ = ln_stats(x.astype(F32) + pe_ref[...].astype(F32))
        low_ref[pl.ds(row, tile), :] = (normed * g_ref[...] + b_ref[...]).astype(BF)

    def loop(i, carry):
        row = pl.multiple_of(i * tile, tile)
        first(row, xm_ref[pl.ds(row, tile), :])
        return carry

    lax.fori_loop(0, whole_tiles, loop, 0)
    first(base, x4_ref[...])
    low_t = low_ref[...].T
    assemble(flat_ref, d4_ref)
    chunk = 256
    for c in range(wide // chunk):
        off = c * chunk
        kind, inner = off // width, off % width
        cur_ref[:base, :] = dm_ref[kind, :, inner : inner + chunk]
        cur_ref[base:, :] = flat_ref[:, off : off + chunk]
        cur = cur_ref[...]
        sums_ref[:, off : off + chunk] = jnp.sum(cur.astype(F32), axis=0, keepdims=True)
        got = dg(low_t, cur, 1, 0).astype(BF)
        at = off
        while at < off + chunk:
            part = at // cols
            end = min(off + chunk, (part + 1) * cols)
            gw_ref[part, :, at - part * cols : end - part * cols] = got[:, at - off : end - off]
            at = end


def wqkv_grad(xm, x4, pe, gain, bias, dm, d4):
    rows_m, width = xm.shape
    rows_4 = x4.shape[0]
    rows = rows_m + rows_4
    parts = d4.shape[0]
    wide = 3 * width
    return pl.pallas_call(
        wqkv_body,
        out_shape=[
            jax.ShapeDtypeStruct((parts, width, wide // parts), BF),
            jax.ShapeDtypeStruct((1, wide), F32),
        ],
        scratch_shapes=[
            pltpu.VMEM((rows, width), BF),
            pltpu.VMEM((rows_4, wide), BF),
            pltpu.VMEM((rows, 256), BF),
        ],
        compiler_params=pltpu.CompilerParams(vmem_limit_bytes=VMEM_LIMIT),
        cost_estimate=cost(2 * rows * width * wide, 2 * (rows * (width + wide) + width * wide)),
        name="wqkv_grad",
    )(xm, x4, pe, gain, bias, dm, d4)


def input_body(xm_ref, x4_ref, pe_ref, g_ref, w_ref, hot_ref, gmm_ref, gm4_ref, dm_ref, d4_ref, gxm_ref, gx4_ref, small_ref, flat_ref):
    tile = pe_ref.shape[0]
    whole_tiles = xm_ref.shape[0] // tile
    base = whole_tiles * tile
    width = xm_ref.shape[1]
    small_ref[...] = jnp.zeros_like(small_ref)
    assemble(flat_ref, d4_ref)

    def finish(x, grad_mixed, up):
        normed, inverse = ln_stats(x.astype(F32) + pe_ref[...].astype(F32))
        small_ref[8:9, :] += jnp.sum(up * normed, axis=0, keepdims=True)
        small_ref[9:10, :] += jnp.sum(up, axis=0, keepdims=True)
        grad = grad_mixed.astype(F32) + ln_back(up, normed, inverse, g_ref[...])
        high = grad.astype(BF)
        rest = (grad - high.astype(F32)).astype(BF)
        small_ref[0:8, :] += dg(hot_ref[...], high, 1, 0) + dg(hot_ref[...], rest, 1, 0)
        return grad

    def loop(i, carry):
        row = pl.multiple_of(i * tile, tile)
        up = dg(dm_ref[0, pl.ds(row, tile), :], w_ref[:, :width], 1, 1)
        up += dg(dm_ref[1, pl.ds(row, tile), :], w_ref[:, width : 2 * width], 1, 1)
        up += dg(dm_ref[2, pl.ds(row, tile), :], w_ref[:, 2 * width :], 1, 1)
        gxm_ref[pl.ds(row, tile), :] = finish(
            xm_ref[pl.ds(row, tile), :], gmm_ref[pl.ds(row, tile), :], up
        ).astype(BF)
        return carry

    lax.fori_loop(0, whole_tiles, loop, 0)
    gx4_ref[...] = finish(x4_ref[...], gm4_ref[...], dg(flat_ref[...], w_ref[...], 1, 1))


def input_grad(xm, x4, pe, gain, w, hot, gmm, gm4, dm, d4):
    rows_m, width = xm.shape
    rows_4 = x4.shape[0]
    rows = rows_m + rows_4
    wide = w.shape[1]
    return pl.pallas_call(
        input_body,
        out_shape=[
            jax.ShapeDtypeStruct((rows_m, width), BF),
            jax.ShapeDtypeStruct((rows_4, width), F32),
            jax.ShapeDtypeStruct((16, width), F32),
        ],
        scratch_shapes=[pltpu.VMEM((rows_4, wide), BF)],
        compiler_params=pltpu.CompilerParams(vmem_limit_bytes=VMEM_LIMIT),
        cost_estimate=cost(2 * rows * width * wide, 2 * (rows * (width + wide) + width * wide)),
        name="input_grad",
    )(xm, x4, pe, gain, w, hot, gmm, gm4, dm, d4)


def swap(value, axis, size, bit):
    return lax.ppermute(value, axis, [(i, i ^ bit) for i in range(size)])


def halve(value, dim, axis, size, bit, last=False):
    mine = (lax.axis_index(axis) // bit) % 2
    keep = lax.dynamic_index_in_dim(value, mine, dim, keepdims=False)
    send = lax.dynamic_index_in_dim(value, 1 - mine, dim, keepdims=False)
    got = swap(send, axis, size, bit)
    total = keep.astype(F32) + got.astype(F32)
    return total if last else total.astype(BF)


def reduce_shard(grad, dp, mix, order):
    _, _, r, c = grad.shape
    if mix != 4 or dp != 8:
        total = lax.psum_scatter(grad, "mix", scatter_dimension=0, tiled=False)
        return lax.psum_scatter(total, "dp", scatter_dimension=0, tiled=False).astype(F32)
    value = grad.reshape(2, 2, 2, 2, 2, r, c)
    names = ["y", "core", "z1", "z0", "x"]
    spots = {"y": ("mix", 4, 2), "core": ("mix", 4, 1), "z1": ("dp", 8, 4), "z0": ("dp", 8, 2), "x": ("dp", 8, 1)}
    for index, name in enumerate(order):
        dim = names.index(name)
        names.pop(dim)
        value = halve(value, dim, *spots[name], last=index == len(order) - 1)
    return value


def sum_all(value, dp, mix):
    for axis, size in (("mix", mix), ("dp", dp)):
        bit = 1
        while bit < size:
            value = value + swap(value, axis, size, bit)
            bit *= 2
    return value


def per_device(
    mix,
    dp,
    inputs,
    pass_count,
    pass_embed,
    ln1_gain,
    ln1_bias,
    w_qkv,
    bias_q,
    bias_v,
    w_out,
    bias_out,
    ln2_gain,
    ln2_bias,
    w_up,
    bias_up,
    w_down,
    bias_down,
    cotangent,
):
    items, slot_dev, width = inputs.shape
    slots = slot_dev * mix
    place = lax.axis_index("mix")
    row = lambda v: v.astype(F32).reshape(1, -1)
    gain1, shift1, gain2, shift2 = row(ln1_gain), row(ln1_bias), row(ln2_gain), row(ln2_bias)

    pass_ids = lax.iota(jnp.int32, slot_dev) % PASSES
    hot = (lax.iota(jnp.int32, 8)[:, None] == pass_ids[None, :]).astype(BF)
    pe = jnp.dot(hot[:PASSES].T, pass_embed, preferred_element_type=F32).astype(BF)
    mine = lax.dynamic_index_in_dim(pass_count, place, keepdims=False)
    other = pass_count[items - 1]
    keep = jnp.stack([pass_ids < mine, pass_ids < other], axis=1).astype(F32)
    slot_pass = lax.iota(jnp.int32, slots) % PASSES
    bias_of = lambda n: jnp.broadcast_to(
        jnp.where(slot_pass < n, 0.0, NEG).astype(F32)[:, None], (slots, TILE)
    )
    kb_m, kb_4 = bias_of(mine), bias_of(other)

    scale = 1.0 / math.sqrt(HEAD)
    joined_bias = jnp.concatenate([row(bias_q), jnp.zeros((1, width), F32), row(bias_v)], axis=1)
    joined_scale = jnp.concatenate(
        [jnp.full((1, width), scale, F32), jnp.ones((1, 2 * width), F32)], axis=1
    )
    piece = width // mix
    regroup = lambda a: a.reshape(-1, 3, mix, piece).transpose(2, 0, 1, 3).reshape(mix, -1, 3 * piece)
    w_split = regroup(w_qkv)
    bias_split = regroup(joined_bias)
    scale_split = jnp.concatenate(
        [jnp.full((1, piece), scale, F32), jnp.ones((1, 2 * piece), F32)], axis=1
    )

    spread = lambda a: lax.all_to_all(a, "mix", 0, 0, tiled=False)

    xm = spread(inputs[: items - 1]).reshape(slots, width)
    cm = spread(cotangent[: items - 1]).reshape(slots, width)
    x4, c4 = inputs[items - 1], cotangent[items - 1]

    qkv4 = spread(qkv_split(x4, pe, gain1, shift1, w_split, bias_split, scale_split))
    qkv4 = qkv4.reshape(slots, 3 * piece)
    qkvm = qkv_whole(xm, pe, gain1, shift1, w_qkv, joined_bias, joined_scale)
    att4h, lse4 = attend_split(qkv4, kb_4)
    att4 = spread(att4h.reshape(mix, slot_dev, piece))
    attm, lsem = attend_whole(qkvm, kb_m)

    outm, out4, gmm, gm4, dam, da4, gwu, gwd, gwo, gbu, small2 = mlp(
        xm,
        x4,
        cm,
        c4,
        attm,
        att4,
        pe,
        keep,
        w_out,
        row(bias_out),
        gain2,
        shift2,
        row(bias_down),
        w_up,
        row(bias_up),
        w_down,
        dp,
    )
    da4h = spread(da4).reshape(slots, piece)
    out_rows = spread(outm.reshape(mix, slot_dev, width))
    wide = w_up.shape[1]
    gwu = gwu.reshape(mix, dp, width // dp, wide // mix)
    if dp == 8:
        pass
    else:
        gwd = gwd.transpose(0, 2, 1, 3).reshape(mix, width // mix, dp, wide // dp).transpose(0, 2, 1, 3)
    gwo = gwo.reshape(mix, dp, width // dp, piece)
    shard_up = reduce_shard(gwu, dp, mix, ["core", "x", "z1", "z0", "y"])
    shard_down = reduce_shard(gwd, dp, mix, ["core", "z1", "z0", "x", "y"]).T
    shard_out = reduce_shard(gwo, dp, mix, ["core", "x", "z1", "z0", "y"])
    small2, gbu = lax.psum((small2, gbu), ("dp", "mix"))

    dm = back_whole(qkvm, dam, attm, lsem, kb_m)
    d4 = back_split(qkv4, da4h, att4h, lse4, kb_4)
    d4 = spread(d4.reshape(mix, slot_dev, 3 * piece))
    gwq, sums = wqkv_grad(xm, x4, pe, gain1, shift1, dm, d4)
    shard_qkv = reduce_shard(
        gwq.reshape(mix, dp, width // dp, 3 * piece), dp, mix, ["core", "x", "z1", "z0", "y"]
    )
    gxm, gx4, small1 = input_grad(xm, x4, pe, gain1, w_qkv, hot, gmm, gm4, dm, d4)
    gx_rows = spread(gxm.reshape(mix, slot_dev, width))
    small1 = sum_all(
        jnp.concatenate([small1[:PASSES], small1[8:10], sums.reshape(3, width)], axis=0), dp, mix
    )

    result = jnp.concatenate([out_rows.astype(F32), out4[None]], axis=0)
    grad_x = jnp.concatenate([gx_rows.astype(F32), gx4[None]], axis=0)
    return (
        result,
        grad_x,
        small1[:PASSES],
        small1[PASSES],
        small1[PASSES + 1],
        shard_qkv,
        small1[PASSES + 2],
        small1[PASSES + 4],
        shard_out,
        small2[3],
        small2[1],
        small2[2],
        shard_up,
        gbu.reshape(-1),
        shard_down,
        small2[0],
    )


def solution(mesh):
    data = P("dp", "mix", None)
    none = P()
    return jax.shard_map(
        functools.partial(per_device, mesh.shape["mix"], mesh.shape["dp"]),
        mesh=mesh,
        in_specs=(data, P("dp")) + (none,) * 14 + (data,),
        out_specs=(
            data,
            data,
            none,
            none,
            none,
            P("dp", "mix"),
            none,
            none,
            P("dp", "mix"),
            none,
            none,
            none,
            P("dp", "mix"),
            none,
            P("dp", "mix"),
            none,
        ),
        check_vma=False,
    )
```
